32 devices in a mesh: inter: 16 (over z, y, x), intra: 2 (over core).
Axes of the slice: x: 2, y: 2, z: 4, core: 2. Of those that a mesh axis runs over, the one named last changes fastest.
Arguments:
- tokens: bfloat16 [2048, 4096], P('inter', 'intra'), may hold values from -6 to 6
- gate_codes: bfloat16 [7168, 4096], P(('intra', 'inter')), may hold values from -127 to 127
- gate_scales: float32 [7168, 16], P(('intra', 'inter')), may hold values from 0.0001 to 0.0005
- up_codes: bfloat16 [7168, 4096], P(('intra', 'inter')), may hold values from -127 to 127
- up_scales: float32 [7168, 16], P(('intra', 'inter')), may hold values from 0.0001 to 0.0005
- cotangent: bfloat16 [2048, 7168], P('inter', 'intra'), may hold values from -6 to 6
Outputs:
- hidden: bfloat16 [2048, 7168], P('inter', 'intra')
- token_grad: bfloat16 [2048, 4096], P('inter', 'intra')
- gate_grad: float32 [7168, 4096], P(('intra', 'inter'))
- up_grad: float32 [7168, 4096], P(('intra', 'inter'))
The draws below stay inside these ranges and needn't reach their ends.
All inputs are finite; a program needn't handle non-finite values.
Results may differ from the reference program's by a relative error of at most 0.02.
Values may be sent and summed in bfloat16 or wider, within the bound.
A program may use at most 384 MiB of HBM per device.

```python
import math
import jax
import jax.numpy as jnp
from jax import lax

D = 4096
FF = 7168
BLOCK = 256
TOK_DEV = 128
TOKENS = 2048
N_INTER = 16
N_INTRA = 2


def draw_gate_codes(key, part):
    values = jax.random.randint(jax.random.fold_in(key, 11), (FF, D), -127, 128)
    return values.astype(jnp.float32).astype(jnp.bfloat16)


def draw_up_codes(key, part):
    values = jax.random.randint(jax.random.fold_in(key, 23), (FF, D), -127, 128)
    return values.astype(jnp.float32).astype(jnp.bfloat16)


def levels(stream_key, extent, pieces, low, high):
    factor_of, own = 1.0, jax.random.fold_in(stream_key, 6)
    for position, parts in pieces:
        steps = jnp.exp(jax.random.uniform(jax.random.fold_in(own, position), (parts,), jnp.float32, low / len(pieces), high / len(pieces)))
        factor_of = factor_of * jnp.repeat(steps, extent[position] // parts).reshape([-1 if axis == position else 1 for axis in range(len(extent))])
    return factor_of


def bell_draw(stream_key, shape, scale, reach, cuts=(), kind=jnp.bfloat16):
    level = levels(stream_key, shape, cuts, -0.22, 0.18) if cuts else 1.0
    entries = jax.random.normal(stream_key, shape, jnp.float32) * scale * level
    return jnp.minimum(jnp.maximum(entries, -reach), reach).astype(kind)


def setup_inputs(seed: int = 0) -> dict:
    seeds = jax.random.split(jax.random.key(seed), 7)
    tokens = bell_draw(seeds[0], (TOKENS, D), 1.0, 6.0, ((0, 16), (1, 2)))
    gate_codes = draw_gate_codes(jax.random.fold_in(seeds[6], 71), 0)
    gate_scales = jnp.clip(jnp.exp(math.log(0.0005) - 1.609438 * jax.random.uniform(seeds[2], (FF, D // BLOCK), jnp.float32) ** levels(seeds[2], (FF, D // BLOCK), ((0, 32),), -0.2, 0.2)), 0.0001, 0.0005)
    up_codes = draw_up_codes(jax.random.fold_in(seeds[6], 71), 0)
    up_scales = jnp.clip(jnp.exp(math.log(0.0005) - 1.609438 * jax.random.uniform(seeds[4], (FF, D // BLOCK), jnp.float32) ** levels(seeds[4], (FF, D // BLOCK), ((0, 32),), -0.2, 0.2)), 0.0001, 0.0005)
    cotangent = bell_draw(seeds[5], (TOKENS, FF), 1.0, 6.0, ((0, 16), (1, 2)))
    return {"tokens": tokens, "gate_codes": gate_codes, "gate_scales": gate_scales, "up_codes": up_codes, "up_scales": up_scales, "cotangent": cotangent}


def dequantize(codes, scales):
    rows, width = codes.shape
    blocks = scales.shape[1]
    values = codes.astype(jnp.float32).reshape(rows, blocks, width // blocks) * scales[:, :, None]
    return values.reshape(rows, width).astype(jnp.bfloat16)


def to_wire(value):
    rounded = value.astype(jnp.bfloat16)
    rounded = lax.optimization_barrier(rounded)
    return rounded.astype(jnp.float32)


def reference(tokens, gate_codes, gate_scales, up_codes, up_scales, cotangent):
    w_gate = dequantize(gate_codes, gate_scales)
    w_up = dequantize(up_codes, up_scales)
    gate = jnp.dot(tokens, w_gate.T, preferred_element_type=jnp.float32)
    up = jnp.dot(tokens, w_up.T, preferred_element_type=jnp.float32)
    sig = jax.nn.sigmoid(gate)
    act = gate * sig
    hidden = (act * up).astype(jnp.bfloat16)
    back = cotangent.astype(jnp.float32)
    d_up = (back * act).astype(jnp.bfloat16)
    d_gate = (back * up * sig * (1.0 + gate * (1.0 - sig))).astype(jnp.bfloat16)
    width = FF // N_INTRA
    total = jnp.zeros((TOKENS, D), jnp.float32)
    for block in range(N_INTRA):
        lower = block * width
        part = jnp.dot(d_gate[:, lower:lower + width], w_gate[lower:lower + width], preferred_element_type=jnp.float32)
        part = part + jnp.dot(d_up[:, lower:lower + width], w_up[lower:lower + width], preferred_element_type=jnp.float32)
        total = total + to_wire(part)
    token_grad = total.astype(jnp.bfloat16)
    grouped_tokens = tokens.reshape(N_INTER, TOK_DEV, D)
    grouped_gate = d_gate.reshape(N_INTER, TOK_DEV, FF)
    grouped_up = d_up.reshape(N_INTER, TOK_DEV, FF)

    def accumulate(carry, group):
        rows, dgs, dus = group
        acc_gate, acc_up = carry
        term_gate = jnp.dot(dgs.T, rows, preferred_element_type=jnp.float32)
        term_up = jnp.dot(dus.T, rows, preferred_element_type=jnp.float32)
        return (acc_gate + to_wire(term_gate), acc_up + to_wire(term_up)), None

    start = (jnp.zeros((FF, D), jnp.float32), jnp.zeros((FF, D), jnp.float32))
    (sum_gate, sum_up), _ = lax.scan(accumulate, start, (grouped_tokens, grouped_gate, grouped_up))
    gate_grad = sum_gate / N_INTER
    up_grad = sum_up / N_INTER
    return hidden, token_grad, gate_grad, up_grad
```

```python
import jax
import jax.numpy as jnp
from jax import lax
from jax.sharding import PartitionSpec as P


def dequantize(codes, scales):
    rows, width = codes.shape
    blocks = scales.shape[1]
    step = width // blocks
    parts = [
        codes[:, b * step:(b + 1) * step].astype(jnp.float32) * scales[:, b:b + 1]
        for b in range(blocks)
    ]
    return jnp.concatenate(parts, axis=1).astype(jnp.bfloat16)


def per_device(tokens, gate_codes, gate_scales, up_codes, up_scales, cotangent):
    groups = lax.axis_size("inter")
    mine = lax.all_gather(tokens, "inter", axis=0, tiled=True)
    whole = lax.all_gather(mine, "intra", axis=0, tiled=False)
    slabs, count, wide = whole.shape
    back = lax.all_to_all(cotangent, "inter", split_axis=1, concat_axis=0, tiled=True)
    w_gate = dequantize(gate_codes, gate_scales)
    w_up = dequantize(up_codes, up_scales)

    def forward(weights):
        total = None
        for s in range(slabs):
            term = lax.dot_general(
                whole[s],
                weights[:, s * wide:(s + 1) * wide],
                (((1,), (1,)), ((), ())),
                preferred_element_type=jnp.float32,
            )
            total = term if total is None else total + term
        return total

    gate = forward(w_gate)
    up = forward(w_up)
    sig = jax.nn.sigmoid(gate)
    act = gate * sig
    hidden = (act * up).astype(jnp.bfloat16)
    back = back.astype(jnp.float32)
    d_up = (back * act).astype(jnp.bfloat16)
    d_gate = (back * up * sig * (1.0 + gate * (1.0 - sig))).astype(jnp.bfloat16)
    hidden = lax.all_to_all(hidden, "inter", split_axis=0, concat_axis=1, tiled=True)

    partial_sum = jnp.dot(d_gate, w_gate, preferred_element_type=jnp.float32)
    partial_sum = partial_sum + jnp.dot(d_up, w_up, preferred_element_type=jnp.float32)
    partial_sum = lax.psum_scatter(
        partial_sum.astype(jnp.bfloat16), "intra", scatter_dimension=1, tiled=True
    )
    token_grad = lax.psum_scatter(partial_sum, "inter", scatter_dimension=0, tiled=True)

    def rows_grad(d_rows):
        terms = [
            lax.dot_general(
                d_rows, whole[s], (((0,), (0,)), ((), ())), preferred_element_type=jnp.float32
            )
            for s in range(slabs)
        ]
        return jnp.concatenate(terms, axis=1) / groups

    return (hidden, token_grad, rows_grad(d_gate), rows_grad(d_up))


def solution(mesh):
    return jax.shard_map(
        per_device,
        mesh=mesh,
        in_specs=(
            P("inter", "intra"),
            P(("intra", "inter"), None),
            P(("intra", "inter"), None),
            P(("intra", "inter"), None),
            P(("intra", "inter"), None),
            P("inter", "intra"),
        ),
        out_specs=(
            P("inter", "intra"),
            P("inter", "intra"),
            P(("intra", "inter"), None),
            P(("intra", "inter"), None),
        ),
        check_vma=False,
    )
```

```python
import functools

import jax
import jax.numpy as jnp
from jax import lax
from jax.experimental import pallas as pl
from jax.experimental.pallas import tpu as pltpu
from jax.sharding import PartitionSpec as P

MESH = pl.DeviceIdType.MESH


def place(groups):
    me = lax.axis_index("inter")
    core = lax.axis_index("intra")
    line = groups // 4
    return me, core, me // 4, line


def bits(me, parity):
    low, high = me % 2, (me // 2) % 2
    a = low * (1 - parity) + high * parity
    b = high * (1 - parity) + low * parity
    return a, b, 1 + parity, 2 - parity


def block_of(z, a, b, stride_a, stride_b):
    return z * 4 + a * stride_a + b * stride_b


def greet(peers):
    barrier = pltpu.get_barrier_semaphore()
    for peer in peers:
        pl.semaphore_signal(barrier, inc=1, device_id=peer, device_id_type=MESH)
    pl.semaphore_wait(barrier, len(peers))


def peers_of(me, core, z, line, cores, a, b, sa, sb):
    to_a = {"inter": block_of(z, 1 - a, b, sa, sb)}
    to_b = {"inter": block_of(z, a, 1 - b, sa, sb)}
    to_z = [{"inter": block_of(lax.rem(z + j, line), a, b, sa, sb)} for j in range(1, line)]
    to_core = [{"intra": lax.rem(core + i, cores)} for i in range(1, cores)]
    return to_a, to_b, to_z, to_core


def gather_kernel(groups, cores, x_ref, out_ref, own_sem, *sems):
    me, core, z, line = place(groups)
    a, b, sa, sb = bits(me, core % 2)
    rows = x_ref.shape[0]
    to_a, to_b, to_z, to_core = peers_of(me, core, z, line, cores, a, b, sa, sb)
    greet([to_a, to_b] + to_z + to_core)
    z_send, z_recv, b_send, b_recv, a_send, a_recv, c_send, c_recv = sems

    def at(slab, block):
        return out_ref.at[slab, pl.ds(pl.multiple_of(block * rows, rows), rows), :]

    started = []

    def send(src, block, send_sem, recv_sem, peer):
        copy = pltpu.make_async_remote_copy(
            src_ref=src, dst_ref=at(core, block), send_sem=send_sem, recv_sem=recv_sem,
            device_id=peer, device_id_type=MESH,
        )
        copy.start()
        started.append(copy)

    def arrived(slab, block, send_sem, recv_sem, peer):
        pltpu.make_async_remote_copy(
            src_ref=x_ref, dst_ref=at(slab, block), send_sem=send_sem, recv_sem=recv_sem,
            device_id=peer, device_id_type=MESH,
        ).wait_recv()

    def to_cores(src, block, slot):
        for i, peer in enumerate(to_core):
            send(src, block, c_send.at[i, slot], c_recv.at[i, slot], peer)

    own = pltpu.make_async_copy(x_ref, at(core, me), own_sem)
    for j in range(1, line):
        send(x_ref, me, z_send.at[j - 1], z_recv.at[j - 1], to_z[j - 1])
    send(x_ref, me, b_send.at[0], b_recv.at[0], to_b)
    send(x_ref, me, a_send.at[0], a_recv.at[0], to_a)
    to_cores(x_ref, me, 0)
    own.start()

    def take_a(j):
        zz = lax.rem(z - j + line, line)
        for k, bb in ((2, b), (3, 1 - b)):
            block = block_of(zz, 1 - a, bb, sa, sb)
            slot = (k - 2) * line + j
            arrived(core, block, a_send.at[slot], a_recv.at[slot], to_a)
            to_cores(at(core, block), block, k * line + j)

    for j in range(line):
        zz = lax.rem(z - j + line, line)
        if j > 0:
            block = block_of(zz, a, b, sa, sb)
            arrived(core, block, z_send.at[j - 1], z_recv.at[j - 1], to_z[j - 1])
            send(at(core, block), block, b_send.at[j], b_recv.at[j], to_b)
            send(at(core, block), block, a_send.at[j], a_recv.at[j], to_a)
            to_cores(at(core, block), block, j)
        block = block_of(zz, a, 1 - b, sa, sb)
        arrived(core, block, b_send.at[j], b_recv.at[j], to_b)
        send(at(core, block), block, a_send.at[line + j], a_recv.at[line + j], to_a)
        to_cores(at(core, block), block, line + j)
        if j > 0:
            take_a(j - 1)
    take_a(line - 1)
    for i in range(1, cores):
        other = lax.rem(core - i + cores, cores)
        oa, ob, osa, osb = bits(me, other % 2)
        for k, (da, db) in enumerate(((0, 0), (0, 1), (1, 0), (1, 1))):
            aa = oa + da - 2 * da * oa
            bb = ob + db - 2 * db * ob
            for j in range(line):
                zz = lax.rem(z - j + line, line)
                block = block_of(zz, aa, bb, osa, osb)
                slot = k * line + j
                arrived(other, block, c_send.at[i - 1, slot], c_recv.at[i - 1, slot], to_core[i - 1])
    own.wait()
    for copy in started:
        copy.wait_send()


def gather_tokens(tokens, groups, cores):
    rows, wide = tokens.shape
    line = groups // 4
    dma = pltpu.SemaphoreType.DMA
    return pl.pallas_call(
        functools.partial(gather_kernel, groups, cores),
        out_shape=jax.ShapeDtypeStruct((cores, groups * rows, wide), tokens.dtype),
        in_specs=[pl.BlockSpec(memory_space=pl.ANY)],
        out_specs=pl.BlockSpec(memory_space=pl.ANY),
        scratch_shapes=[
            dma,
            dma((line - 1,)), dma((line - 1,)),
            dma((line,)), dma((line,)),
            dma((2 * line,)), dma((2 * line,)),
            dma((cores - 1, 4 * line)), dma((cores - 1, 4 * line)),
        ],
        compiler_params=pltpu.CompilerParams(collective_id=0, has_side_effects=True),
        name="gather_tokens",
    )(tokens)


def scatter_kernel(groups, cores, x_ref, out_ref, acc, from_core, from_a, from_b, from_z, *sems):
    me, core, z, line = place(groups)
    a, b, sa, sb = bits(me, core % 2)
    rows, wide = out_ref.shape
    to_a, to_b, to_z, to_core = peers_of(me, core, z, line, cores, a, b, sa, sb)
    greet([to_a, to_b] + to_z + to_core)
    own_sem, c_send, c_recv, a_send, a_recv, b_send, b_recv, z_send, z_recv = sems

    def block_at(parity, k, j):
        pa, pb, psa, psb = bits(me, parity)
        aa = 1 - pa if k < 2 else pa
        bb = 1 - pb if k % 2 == 0 else pb
        return block_of(lax.rem(z + 1 + j, line), aa, bb, psa, psb)

    def part(block, slab):
        return x_ref.at[
            pl.ds(pl.multiple_of(block * rows, rows), rows),
            pl.ds(pl.multiple_of(slab * wide, wide), wide),
        ]

    started, loads = [], {}

    def remote(src, dst, send_sem, recv_sem, peer):
        return pltpu.make_async_remote_copy(
            src_ref=src, dst_ref=dst, send_sem=send_sem, recv_sem=recv_sem,
            device_id=peer, device_id_type=MESH,
        )

    def send(*args):
        copy = remote(*args)
        copy.start()
        started.append(copy)

    for k in range(4):
        for j in range(line):
            slot = k * line + j
            for i in range(1, cores):
                other = lax.rem(core + i, cores)
                block = block_at(other % 2, k, j)
                send(part(block, other), from_core.at[i - 1, slot], c_send.at[i - 1, slot],
                     c_recv.at[i - 1, slot], to_core[i - 1])
            loads[slot] = pltpu.make_async_copy(
                part(block_at(core % 2, k, j), core), acc.at[slot], own_sem.at[slot])
            loads[slot].start()

    def group_sum(slot, extras):
        loads[slot].wait()
        for i in range(cores - 1):
            remote(acc.at[slot], from_core.at[i, slot], c_send.at[i, slot], c_recv.at[i, slot],
                   to_core[i]).wait_recv()
        refs = [acc.at[slot]] + [from_core.at[i, slot] for i in range(cores - 1)] + extras
        return refs

    def add(refs, dst):
        step = 16

        def body(r, _):
            here = pl.ds(pl.multiple_of(r * step, step), step)
            total = refs[0][here, :].astype(jnp.float32)
            for ref in refs[1:]:
                total = total + ref[here, :].astype(jnp.float32)
            dst[here, :] = total.astype(dst.dtype)
            return 0

        lax.fori_loop(0, rows // step, body, 0)

    for slot in range(2 * line):
        add(group_sum(slot, []), acc.at[slot])
        send(acc.at[slot], from_a.at[slot], a_send.at[slot], a_recv.at[slot], to_a)
    for j in range(line):
        slot = 2 * line + j
        refs = group_sum(slot, [from_a.at[j]])
        remote(acc.at[slot], from_a.at[j], a_send.at[j], a_recv.at[j], to_a).wait_recv()
        add(refs, acc.at[slot])
        send(acc.at[slot], from_b.at[j], b_send.at[j], b_recv.at[j], to_b)
    for j in range(line):
        slot = 3 * line + j
        refs = group_sum(slot, [from_a.at[line + j], from_b.at[j]])
        remote(acc.at[slot], from_a.at[line + j], a_send.at[line + j], a_recv.at[line + j],
               to_a).wait_recv()
        remote(acc.at[slot], from_b.at[j], b_send.at[j], b_recv.at[j], to_b).wait_recv()
        if j < line - 1:
            add(refs, acc.at[slot])
            send(acc.at[slot], from_z.at[j], z_send.at[j], z_recv.at[j], to_z[j])
        else:
            for i in range(line - 1):
                remote(acc.at[slot], from_z.at[i], z_send.at[i], z_recv.at[i], to_z[i]).wait_recv()
            add(refs + [from_z.at[i] for i in range(line - 1)], out_ref)
    for copy in started:
        copy.wait_send()


def scatter_sum(partial_sum, groups, cores):
    tokens, width = partial_sum.shape
    rows, wide, line = tokens // groups, width // cores, groups // 4
    dma = pltpu.SemaphoreType.DMA

    def slots(*count):
        return pltpu.VMEM((*count, rows, wide), partial_sum.dtype)

    return pl.pallas_call(
        functools.partial(scatter_kernel, groups, cores),
        out_shape=jax.ShapeDtypeStruct((rows, wide), partial_sum.dtype),
        in_specs=[pl.BlockSpec(memory_space=pl.ANY)],
        out_specs=pl.BlockSpec(memory_space=pltpu.VMEM),
        scratch_shapes=[
            slots(4 * line), slots(cores - 1, 4 * line), slots(2 * line), slots(line),
            slots(line - 1),
            dma((4 * line,)),
            dma((cores - 1, 4 * line)), dma((cores - 1, 4 * line)),
            dma((2 * line,)), dma((2 * line,)),
            dma((line,)), dma((line,)),
            dma((line - 1,)), dma((line - 1,)),
        ],
        compiler_params=pltpu.CompilerParams(collective_id=1, has_side_effects=True),
        name="scatter_sum",
    )(partial_sum)


def dequantize(codes, scales):
    rows, width = codes.shape
    blocks = scales.shape[1]
    step = width // blocks
    parts = [
        codes[:, b * step:(b + 1) * step].astype(jnp.float32) * scales[:, b:b + 1]
        for b in range(blocks)
    ]
    return jnp.concatenate(parts, axis=1).astype(jnp.bfloat16)


def per_device(tokens, gate_codes, gate_scales, up_codes, up_scales, cotangent):
    groups = lax.axis_size("inter")
    whole = gather_tokens(tokens, groups, lax.axis_size("intra"))
    slabs, count, wide = whole.shape
    back = lax.all_to_all(cotangent, "inter", split_axis=1, concat_axis=0, tiled=True)
    w_gate = dequantize(gate_codes, gate_scales)
    w_up = dequantize(up_codes, up_scales)

    def forward(weights):
        total = None
        for s in range(slabs):
            term = lax.dot_general(
                whole[s],
                weights[:, s * wide:(s + 1) * wide],
                (((1,), (1,)), ((), ())),
                preferred_element_type=jnp.float32,
            )
            total = term if total is None else total + term
        return total

    gate = forward(w_gate)
    up = forward(w_up)
    sig = jax.nn.sigmoid(gate)
    act = gate * sig
    hidden = (act * up).astype(jnp.bfloat16)
    back = back.astype(jnp.float32)
    d_up = (back * act).astype(jnp.bfloat16)
    d_gate = (back * up * sig * (1.0 + gate * (1.0 - sig))).astype(jnp.bfloat16)
    hidden = lax.all_to_all(hidden, "inter", split_axis=0, concat_axis=1, tiled=True)

    partial_sum = jnp.dot(d_gate, w_gate, preferred_element_type=jnp.float32)
    partial_sum = partial_sum + jnp.dot(d_up, w_up, preferred_element_type=jnp.float32)
    token_grad = scatter_sum(
        partial_sum.astype(jnp.bfloat16), groups, lax.axis_size("intra")
    )

    def rows_grad(d_rows):
        terms = [
            lax.dot_general(
                d_rows, whole[s], (((0,), (0,)), ((), ())), preferred_element_type=jnp.float32
            )
            for s in range(slabs)
        ]
        return jnp.concatenate(terms, axis=1) / groups

    return (hidden, token_grad, rows_grad(d_gate), rows_grad(d_up))


def solution(mesh):
    return jax.shard_map(
        per_device,
        mesh=mesh,
        in_specs=(
            P("inter", "intra"),
            P(("intra", "inter"), None),
            P(("intra", "inter"), None),
            P(("intra", "inter"), None),
            P(("intra", "inter"), None),
            P("inter", "intra"),
        ),
        out_specs=(
            P("inter", "intra"),
            P("inter", "intra"),
            P(("intra", "inter"), None),
            P(("intra", "inter"), None),
        ),
        check_vma=False,
    )
```

```python
import functools

import jax
import jax.numpy as jnp
from jax import lax
from jax.experimental import pallas as pl
from jax.experimental.pallas import tpu as pltpu
from jax.sharding import PartitionSpec as P

MESH = pl.DeviceIdType.MESH


def place(groups):
    me = lax.axis_index("inter")
    core = lax.axis_index("intra")
    line = groups // 4
    return me, core, me // 4, line


def bits(me, parity):
    low, high = me % 2, (me // 2) % 2
    a = low * (1 - parity) + high * parity
    b = high * (1 - parity) + low * parity
    return a, b, 1 + parity, 2 - parity


def block_of(z, a, b, stride_a, stride_b):
    return z * 4 + a * stride_a + b * stride_b


def greet(peers):
    barrier = pltpu.get_barrier_semaphore()
    for peer in peers:
        pl.semaphore_signal(barrier, inc=1, device_id=peer, device_id_type=MESH)
    pl.semaphore_wait(barrier, len(peers))


def peers_of(me, core, z, line, cores, a, b, sa, sb):
    to_a = {"inter": block_of(z, 1 - a, b, sa, sb)}
    to_b = {"inter": block_of(z, a, 1 - b, sa, sb)}
    to_z = [{"inter": block_of(lax.rem(z + j, line), a, b, sa, sb)} for j in range(1, line)]
    to_core = [{"intra": lax.rem(core + i, cores)} for i in range(1, cores)]
    return to_a, to_b, to_z, to_core


def gather_kernel(groups, cores, x_ref, gc_ref, gs_ref, uc_ref, us_ref, out_ref, w_ref, own_sem, *sems):
    me, core, z, line = place(groups)
    a, b, sa, sb = bits(me, core % 2)
    rows = x_ref.shape[0]
    to_a, to_b, to_z, to_core = peers_of(me, core, z, line, cores, a, b, sa, sb)
    greet([to_a, to_b] + to_z + to_core)
    z_send, z_recv, b_send, b_recv, a_send, a_recv, c_send, c_recv = sems

    def at(slab, block):
        return out_ref.at[slab, pl.ds(pl.multiple_of(block * rows, rows), rows), :]

    started = []

    def send(src, block, send_sem, recv_sem, peer):
        copy = pltpu.make_async_remote_copy(
            src_ref=src, dst_ref=at(core, block), send_sem=send_sem, recv_sem=recv_sem,
            device_id=peer, device_id_type=MESH,
        )
        copy.start()
        started.append(copy)

    def arrived(slab, block, send_sem, recv_sem, peer):
        pltpu.make_async_remote_copy(
            src_ref=x_ref, dst_ref=at(slab, block), send_sem=send_sem, recv_sem=recv_sem,
            device_id=peer, device_id_type=MESH,
        ).wait_recv()

    def to_cores(src, block, slot):
        for i, peer in enumerate(to_core):
            send(src, block, c_send.at[i, slot], c_recv.at[i, slot], peer)

    own = pltpu.make_async_copy(x_ref, at(core, me), own_sem)
    for j in range(1, line):
        send(x_ref, me, z_send.at[j - 1], z_recv.at[j - 1], to_z[j - 1])
    send(x_ref, me, b_send.at[0], b_recv.at[0], to_b)
    send(x_ref, me, a_send.at[0], a_recv.at[0], to_a)
    to_cores(x_ref, me, 0)
    own.start()

    owned, blocks = gs_ref.shape
    step = gc_ref.shape[1] // blocks
    for first, codes, scales in ((0, gc_ref, gs_ref), (owned, uc_ref, us_ref)):
        for blk in range(blocks):
            values = codes[:, blk * step:(blk + 1) * step].astype(jnp.float32)
            values = values * scales[:, blk:blk + 1]
            w_ref[first:first + owned, blk * step:(blk + 1) * step] = values.astype(w_ref.dtype)

    def take_a(j):
        zz = lax.rem(z - j + line, line)
        for k, bb in ((2, b), (3, 1 - b)):
            block = block_of(zz, 1 - a, bb, sa, sb)
            slot = (k - 2) * line + j
            arrived(core, block, a_send.at[slot], a_recv.at[slot], to_a)
            to_cores(at(core, block), block, k * line + j)

    for j in range(line):
        zz = lax.rem(z - j + line, line)
        if j > 0:
            block = block_of(zz, a, b, sa, sb)
            arrived(core, block, z_send.at[j - 1], z_recv.at[j - 1], to_z[j - 1])
            send(at(core, block), block, b_send.at[j], b_recv.at[j], to_b)
            send(at(core, block), block, a_send.at[j], a_recv.at[j], to_a)
            to_cores(at(core, block), block, j)
        block = block_of(zz, a, 1 - b, sa, sb)
        arrived(core, block, b_send.at[j], b_recv.at[j], to_b)
        send(at(core, block), block, a_send.at[line + j], a_recv.at[line + j], to_a)
        to_cores(at(core, block), block, line + j)
        if j > 0:
            take_a(j - 1)
    take_a(line - 1)
    for i in range(1, cores):
        other = lax.rem(core - i + cores, cores)
        oa, ob, osa, osb = bits(me, other % 2)
        for k, (da, db) in enumerate(((0, 0), (0, 1), (1, 0), (1, 1))):
            aa = oa + da - 2 * da * oa
            bb = ob + db - 2 * db * ob
            for j in range(line):
                zz = lax.rem(z - j + line, line)
                block = block_of(zz, aa, bb, osa, osb)
                slot = k * line + j
                arrived(other, block, c_send.at[i - 1, slot], c_recv.at[i - 1, slot], to_core[i - 1])
    own.wait()
    for copy in started:
        copy.wait_send()


def gather_tokens(tokens, gate_codes, gate_scales, up_codes, up_scales, groups, cores):
    rows, wide = tokens.shape
    line = groups // 4
    dma = pltpu.SemaphoreType.DMA
    return pl.pallas_call(
        functools.partial(gather_kernel, groups, cores),
        out_shape=(
            jax.ShapeDtypeStruct((cores, groups * rows, wide), tokens.dtype),
            jax.ShapeDtypeStruct((2 * gate_codes.shape[0], gate_codes.shape[1]), jnp.bfloat16),
        ),
        in_specs=[pl.BlockSpec(memory_space=pl.ANY)] + [pl.BlockSpec(memory_space=pltpu.VMEM)] * 4,
        out_specs=(
            pl.BlockSpec(memory_space=pl.ANY), pl.BlockSpec(memory_space=pltpu.VMEM),
        ),
        scratch_shapes=[
            dma,
            dma((line - 1,)), dma((line - 1,)),
            dma((line,)), dma((line,)),
            dma((2 * line,)), dma((2 * line,)),
            dma((cores - 1, 4 * line)), dma((cores - 1, 4 * line)),
        ],
        compiler_params=pltpu.CompilerParams(collective_id=0, has_side_effects=True),
        name="gather_tokens",
    )(tokens, gate_codes, gate_scales, up_codes, up_scales)


def scatter_kernel(groups, cores, d_ref, w_ref, h_ref, out_ref, hid_ref, sums, outbox,
                   from_core, from_a, from_b, from_z, *sems):
    me, core, z, line = place(groups)
    a, b, sa, sb = bits(me, core % 2)
    rows, wide = out_ref.shape
    to_a, to_b, to_z, to_core = peers_of(me, core, z, line, cores, a, b, sa, sb)
    to_all = [{"inter": lax.rem(me + i, groups)} for i in range(1, groups)]
    greet(to_all + to_core)
    (c_send, c_recv, a_send, a_recv, b_send, b_recv, z_send, z_recv, h_send, h_recv,
     h_own) = sems
    ring = outbox.shape[0]
    tile = min(512, wide)

    def block_at(parity, k, j):
        pa, pb, psa, psb = bits(me, parity)
        aa = 1 - pa if k < 2 else pa
        bb = 1 - pb if k % 2 == 0 else pb
        return block_of(lax.rem(z + 1 + j, line), aa, bb, psa, psb)

    started = []

    def remote(src, dst, send_sem, recv_sem, peer):
        return pltpu.make_async_remote_copy(
            src_ref=src, dst_ref=dst, send_sem=send_sem, recv_sem=recv_sem,
            device_id=peer, device_id_type=MESH,
        )

    def send(*args):
        copy = remote(*args)
        copy.start()
        started.append(copy)

    def add(block, slab, refs, dst):
        here = pl.ds(pl.multiple_of(block * rows, rows), rows)

        def body(t, _):
            cols = pl.ds(pl.multiple_of(t * tile, tile), tile)
            total = jnp.dot(
                d_ref[here, :],
                w_ref[:, pl.ds(pl.multiple_of(slab * wide + t * tile, tile), tile)],
                preferred_element_type=jnp.float32,
            )
            for ref in refs:
                total = total + ref[:, cols].astype(jnp.float32)
            dst[:, cols] = total.astype(dst.dtype)
            return 0

        lax.fori_loop(0, wide // tile, body, 0)

    pending = {}

    def give(slot):
        k, j = slot // line, slot % line
        for i in range(1, cores):
            other = lax.rem(core + i, cores)
            box = outbox.at[slot % ring, i - 1]
            if (slot % ring, i) in pending:
                pending[slot % ring, i].wait_send()
            add(block_at(other % 2, k, j), other, [], box)
            copy = remote(box, from_core.at[i - 1, slot], c_send.at[i - 1, slot],
                          c_recv.at[i - 1, slot], to_core[i - 1])
            copy.start()
            pending[slot % ring, i] = copy

    def own(slot):
        return block_at(core % 2, slot // line, slot % line)

    def given(slot):
        for i in range(cores - 1):
            remote(outbox.at[0, i], from_core.at[i, slot], c_send.at[i, slot], c_recv.at[i, slot],
                   to_core[i]).wait_recv()
        return [from_core.at[i, slot] for i in range(cores - 1)]

    def hidden_of(block):
        return h_ref.at[pl.ds(pl.multiple_of(block * rows, rows), rows), :]

    give(0)
    give(1)
    for slot in range(2 * line):
        for later in (2 * slot + 2, 2 * slot + 3):
            if later < 4 * line:
                give(later)
        add(own(slot), core, given(slot), sums.at[slot])
        send(sums.at[slot], from_a.at[slot], a_send.at[slot], a_recv.at[slot], to_a)
    for i in range(1, groups):
        peer = lax.rem(me + i, groups)
        send(hidden_of(peer), hid_ref.at[me], h_send.at[i - 1], h_recv.at[i - 1], to_all[i - 1])
    kept = pltpu.make_async_copy(hidden_of(me), hid_ref.at[me], h_own)
    kept.start()
    for j in range(line):
        slot = 2 * line + j
        refs = given(slot) + [from_a.at[j]]
        remote(sums.at[slot], from_a.at[j], a_send.at[j], a_recv.at[j], to_a).wait_recv()
        add(own(slot), core, refs, sums.at[slot])
        send(sums.at[slot], from_b.at[j], b_send.at[j], b_recv.at[j], to_b)
    for j in range(line):
        slot = 3 * line + j
        refs = given(slot) + [from_a.at[line + j], from_b.at[j]]
        remote(sums.at[slot], from_a.at[line + j], a_send.at[line + j], a_recv.at[line + j],
               to_a).wait_recv()
        remote(sums.at[slot], from_b.at[j], b_send.at[j], b_recv.at[j], to_b).wait_recv()
        if j < line - 1:
            add(own(slot), core, refs, sums.at[slot])
            send(sums.at[slot], from_z.at[j], z_send.at[j], z_recv.at[j], to_z[j])
        else:
            for i in range(line - 1):
                remote(sums.at[slot], from_z.at[i], z_send.at[i], z_recv.at[i], to_z[i]).wait_recv()
            add(own(slot), core, refs + [from_z.at[i] for i in range(line - 1)], out_ref)
    for i in range(1, groups):
        peer = lax.rem(me - i + groups, groups)
        remote(hidden_of(me), hid_ref.at[peer], h_send.at[i - 1], h_recv.at[i - 1],
               to_all[i - 1]).wait_recv()
    kept.wait()
    for copy in started + list(pending.values()):
        copy.wait_send()


def scatter_sum(d_both, w_both, hidden, groups, cores):
    tokens, width = d_both.shape[0], w_both.shape[1]
    rows, wide, line = tokens // groups, width // cores, groups // 4
    dma = pltpu.SemaphoreType.DMA

    def slots(*count):
        return pltpu.VMEM((*count, rows, wide), jnp.bfloat16)

    return pl.pallas_call(
        functools.partial(scatter_kernel, groups, cores),
        out_shape=(
            jax.ShapeDtypeStruct((rows, wide), jnp.bfloat16),
            jax.ShapeDtypeStruct((groups, rows, hidden.shape[1]), hidden.dtype),
        ),
        in_specs=[
            pl.BlockSpec(memory_space=pltpu.VMEM), pl.BlockSpec(memory_space=pltpu.VMEM),
            pl.BlockSpec(memory_space=pl.ANY),
        ],
        out_specs=(
            pl.BlockSpec(memory_space=pltpu.VMEM), pl.BlockSpec(memory_space=pl.ANY),
        ),
        scratch_shapes=[
            slots(4 * line), slots(4, cores - 1), slots(cores - 1, 4 * line), slots(2 * line),
            slots(line), slots(line - 1),
            dma((cores - 1, 4 * line)), dma((cores - 1, 4 * line)),
            dma((2 * line,)), dma((2 * line,)),
            dma((line,)), dma((line,)),
            dma((line - 1,)), dma((line - 1,)),
            dma((groups - 1,)), dma((groups - 1,)), dma,
        ],
        compiler_params=pltpu.CompilerParams(collective_id=1, has_side_effects=True),
        name="scatter_sum",
    )(d_both, w_both, hidden)


def per_device(tokens, gate_codes, gate_scales, up_codes, up_scales, cotangent):
    groups = lax.axis_size("inter")
    whole, w_both = gather_tokens(
        tokens, gate_codes, gate_scales, up_codes, up_scales, groups, lax.axis_size("intra")
    )
    slabs, count, wide = whole.shape
    back = lax.all_to_all(cotangent, "inter", split_axis=1, concat_axis=0, tiled=True)
    owned = gate_codes.shape[0]

    def forward(weights):
        total = None
        for s in range(slabs):
            term = lax.dot_general(
                whole[s],
                weights[:, s * wide:(s + 1) * wide],
                (((1,), (1,)), ((), ())),
                preferred_element_type=jnp.float32,
            )
            total = term if total is None else total + term
        return total

    gate = forward(w_both[:owned])
    up = forward(w_both[owned:])
    sig = jax.nn.sigmoid(gate)
    act = gate * sig
    hidden = (act * up).astype(jnp.bfloat16)
    back = back.astype(jnp.float32)
    d_up = (back * act).astype(jnp.bfloat16)
    d_gate = (back * up * sig * (1.0 + gate * (1.0 - sig))).astype(jnp.bfloat16)
    token_grad, parts = scatter_sum(
        jnp.concatenate([d_gate, d_up], axis=1), w_both, hidden, groups, lax.axis_size("intra")
    )
    hidden = parts.transpose(1, 0, 2).reshape(parts.shape[1], groups * owned)

    def rows_grad(d_rows):
        terms = [
            lax.dot_general(
                d_rows, whole[s], (((0,), (0,)), ((), ())), preferred_element_type=jnp.float32
            )
            for s in range(slabs)
        ]
        return jnp.concatenate(terms, axis=1) / groups

    return (hidden, token_grad, rows_grad(d_gate), rows_grad(d_up))


def solution(mesh):
    return jax.shard_map(
        per_device,
        mesh=mesh,
        in_specs=(
            P("inter", "intra"),
            P(("intra", "inter"), None),
            P(("intra", "inter"), None),
            P(("intra", "inter"), None),
            P(("intra", "inter"), None),
            P("inter", "intra"),
        ),
        out_specs=(
            P("inter", "intra"),
            P("inter", "intra"),
            P(("intra", "inter"), None),
            P(("intra", "inter"), None),
        ),
        check_vma=False,
    )
```

```python
import functools

import jax
import jax.numpy as jnp
from jax import lax
from jax.experimental import pallas as pl
from jax.experimental.pallas import tpu as pltpu
from jax.sharding import PartitionSpec as P

MESH = pl.DeviceIdType.MESH


def place(groups):
    me = lax.axis_index("inter")
    core = lax.axis_index("intra")
    line = groups // 4
    return me, core, me // 4, line


def bits(me, parity):
    low, high = me % 2, (me // 2) % 2
    a = low * (1 - parity) + high * parity
    b = high * (1 - parity) + low * parity
    return a, b, 1 + parity, 2 - parity


def block_of(z, a, b, stride_a, stride_b):
    return z * 4 + a * stride_a + b * stride_b


def greet(peers):
    barrier = pltpu.get_barrier_semaphore()
    for peer in peers:
        pl.semaphore_signal(barrier, inc=1, device_id=peer, device_id_type=MESH)
    pl.semaphore_wait(barrier, len(peers))


def peers_of(me, core, z, line, cores, a, b, sa, sb):
    to_a = {"inter": block_of(z, 1 - a, b, sa, sb)}
    to_b = {"inter": block_of(z, a, 1 - b, sa, sb)}
    to_z = [{"inter": block_of(lax.rem(z + j, line), a, b, sa, sb)} for j in range(1, line)]
    to_core = [{"intra": lax.rem(core + i, cores)} for i in range(1, cores)]
    return to_a, to_b, to_z, to_core


def gather_kernel(groups, cores, x_ref, gc_ref, gs_ref, uc_ref, us_ref, out_ref, w_ref, own_sem, *sems):
    me, core, z, line = place(groups)
    a, b, sa, sb = bits(me, core % 2)
    rows = x_ref.shape[0]
    to_a, to_b, to_z, to_core = peers_of(me, core, z, line, cores, a, b, sa, sb)
    greet([to_a, to_b] + to_z + to_core)
    up_send, down_send, z_recv, b_send, b_recv, a_send, a_recv, c_send, c_recv = sems

    def at(slab, block):
        return out_ref.at[slab, pl.ds(pl.multiple_of(block * rows, rows), rows), :]

    def copy_of(src, slab, block, send_sem, recv_sem, peer):
        return pltpu.make_async_remote_copy(
            src_ref=src, dst_ref=at(slab, block), send_sem=send_sem, recv_sem=recv_sem,
            device_id=peer, device_id_type=MESH,
        )

    def block(k, zz, parity=None):
        pa, pb, psa, psb = bits(me, core % 2 if parity is None else parity)
        return block_of(zz, 1 - pa if k >= 2 else pa, 1 - pb if k % 2 else pb, psa, psb)

    up = {"inter": block_of(lax.rem(z + 1, line), a, b, sa, sb)}
    down = {"inter": block_of(lax.rem(z - 1 + line, line), a, b, sa, sb)}

    def to_a_copy(src, k, zz):
        return copy_of(src, core, block(k, zz), a_send.at[k, zz], a_recv.at[k, zz], to_a)

    def to_b_copy(src, zz):
        return copy_of(src, core, block(0, zz), b_send.at[zz], b_recv.at[zz], to_b)

    def core_copies(src, k, zz):
        return [
            copy_of(src, core, block(k, zz), c_send.at[i, k, zz], c_recv.at[i, k, zz], peer)
            for i, peer in enumerate(to_core)
        ]

    def line_copy(src, zz, upward):
        sems_of, peer = (up_send, up) if upward else (down_send, down)
        return copy_of(src, core, block(0, zz), sems_of.at[zz], z_recv.at[zz], peer)

    def begin(copies):
        for copy in copies:
            copy.start()

    own = pltpu.make_async_copy(x_ref, at(core, me), own_sem)

    @pl.when(z < line - 1)
    def _():
        line_copy(x_ref, z, True).start()

    @pl.when(z > 0)
    def _():
        line_copy(x_ref, z, False).start()

    begin([to_b_copy(x_ref, z), to_a_copy(x_ref, 0, z)] + core_copies(x_ref, 0, z))
    own.start()

    owned, blocks = gs_ref.shape
    step = gc_ref.shape[1] // blocks
    for first, codes, scales in ((0, gc_ref, gs_ref), (owned, uc_ref, us_ref)):
        for blk in range(blocks):
            values = codes[:, blk * step:(blk + 1) * step].astype(jnp.float32)
            values = values * scales[:, blk:blk + 1]
            w_ref[first:first + owned, blk * step:(blk + 1) * step] = values.astype(w_ref.dtype)

    def take_b(zz):
        src = at(core, block(1, zz))
        copy_of(x_ref, core, block(1, zz), b_send.at[zz], b_recv.at[zz], to_b).wait_recv()
        begin([to_a_copy(src, 1, zz)] + core_copies(src, 1, zz))

    def take_a(zz):
        for k in (2, 3):
            src = at(core, block(k, zz))
            copy_of(x_ref, core, block(k, zz), a_send.at[k - 2, zz], a_recv.at[k - 2, zz],
                    to_a).wait_recv()
            begin(core_copies(src, k, zz))

    def take_line(zz, upward):
        src = at(core, block(0, zz))
        line_copy(x_ref, zz, upward).wait_recv()

        @pl.when(z < line - 1 if upward else z > 0)
        def _():
            line_copy(src, zz, upward).start()

        begin([to_b_copy(src, zz), to_a_copy(src, 0, zz)] + core_copies(src, 0, zz))

    def nearby(shift, act):
        @pl.when(z >= shift)
        def _():
            act(z - shift, True)

        @pl.when(z + shift < line)
        def _():
            act(z + shift, False)

    take_b(z)
    for shift in range(1, line):
        nearby(shift, take_line)
        if shift == 1:
            take_a(z)
        else:
            nearby(shift - 1, lambda zz, _: take_a(zz))
        nearby(shift, lambda zz, _: take_b(zz))
    if line == 1:
        take_a(z)
    else:
        nearby(line - 1, lambda zz, _: take_a(zz))
    for i in range(1, cores):
        other = lax.rem(core - i + cores, cores)
        for k in range(4):
            for zz in range(line):
                copy_of(x_ref, other, block(k, zz, other % 2), c_send.at[i - 1, k, zz],
                        c_recv.at[i - 1, k, zz], to_core[i - 1]).wait_recv()
    own.wait()
    for zz in range(line):
        to_b_copy(x_ref, zz).wait_send()
        for k in range(2):
            to_a_copy(x_ref, k, zz).wait_send()
        for k in range(4):
            for copy in core_copies(x_ref, k, zz):
                copy.wait_send()

        @pl.when((zz <= z) & (z < line - 1))
        def _():
            line_copy(x_ref, zz, True).wait_send()

        @pl.when((zz >= z) & (z > 0))
        def _():
            line_copy(x_ref, zz, False).wait_send()


def gather_tokens(tokens, gate_codes, gate_scales, up_codes, up_scales, groups, cores):
    rows, wide = tokens.shape
    line = groups // 4
    dma = pltpu.SemaphoreType.DMA
    return pl.pallas_call(
        functools.partial(gather_kernel, groups, cores),
        out_shape=(
            jax.ShapeDtypeStruct((cores, groups * rows, wide), tokens.dtype),
            jax.ShapeDtypeStruct((2 * gate_codes.shape[0], gate_codes.shape[1]), jnp.bfloat16),
        ),
        in_specs=[pl.BlockSpec(memory_space=pl.ANY)] + [pl.BlockSpec(memory_space=pltpu.VMEM)] * 4,
        out_specs=(
            pl.BlockSpec(memory_space=pl.ANY), pl.BlockSpec(memory_space=pltpu.VMEM),
        ),
        scratch_shapes=[
            dma,
            dma((line,)), dma((line,)), dma((line,)),
            dma((line,)), dma((line,)),
            dma((2, line)), dma((2, line)),
            dma((cores - 1, 4, line)), dma((cores - 1, 4, line)),
        ],
        compiler_params=pltpu.CompilerParams(collective_id=0, has_side_effects=True),
        name="gather_tokens",
    )(tokens, gate_codes, gate_scales, up_codes, up_scales)


def scatter_kernel(groups, cores, d_ref, w_ref, h_ref, out_ref, hid_ref, sums, outbox,
                   from_core, from_a, from_b, from_z, *sems):
    me, core, z, line = place(groups)
    a, b, sa, sb = bits(me, core % 2)
    rows, wide = out_ref.shape
    to_a, to_b, to_z, to_core = peers_of(me, core, z, line, cores, a, b, sa, sb)
    to_all = [{"inter": lax.rem(me + i, groups)} for i in range(1, groups)]
    greet(to_all + to_core)
    (c_send, c_recv, a_send, a_recv, b_send, b_recv, z_send, z_recv, h_send, h_recv,
     h_own) = sems
    ring = outbox.shape[0]
    tile = min(512, wide)

    def block_at(parity, k, j):
        pa, pb, psa, psb = bits(me, parity)
        aa = 1 - pa if k < 2 else pa
        bb = 1 - pb if k % 2 == 0 else pb
        return block_of(lax.rem(z + 1 + j, line), aa, bb, psa, psb)

    started = []

    def remote(src, dst, send_sem, recv_sem, peer):
        return pltpu.make_async_remote_copy(
            src_ref=src, dst_ref=dst, send_sem=send_sem, recv_sem=recv_sem,
            device_id=peer, device_id_type=MESH,
        )

    def send(*args):
        copy = remote(*args)
        copy.start()
        started.append(copy)

    def add(block, slab, refs, dst):
        here = pl.ds(pl.multiple_of(block * rows, rows), rows)

        def body(t, _):
            cols = pl.ds(pl.multiple_of(t * tile, tile), tile)
            total = jnp.dot(
                d_ref[here, :],
                w_ref[:, pl.ds(pl.multiple_of(slab * wide + t * tile, tile), tile)],
                preferred_element_type=jnp.float32,
            )
            for ref in refs:
                total = total + ref[:, cols].astype(jnp.float32)
            dst[:, cols] = total.astype(dst.dtype)
            return 0

        lax.fori_loop(0, wide // tile, body, 0)

    pending = {}

    def give(slot, n):
        k, j = slot // line, slot % line
        for i in range(1, cores):
            other = lax.rem(core + i, cores)
            box = outbox.at[n % ring, i - 1]
            if (n % ring, i) in pending:
                pending[n % ring, i].wait_send()
            add(block_at(other % 2, k, j), other, [], box)
            copy = remote(box, from_core.at[i - 1, slot], c_send.at[i - 1, slot],
                          c_recv.at[i - 1, slot], to_core[i - 1])
            copy.start()
            pending[n % ring, i] = copy

    def own(slot):
        return block_at(core % 2, slot // line, slot % line)

    def given(slot):
        for i in range(cores - 1):
            remote(outbox.at[0, i], from_core.at[i, slot], c_send.at[i, slot], c_recv.at[i, slot],
                   to_core[i]).wait_recv()
        return [from_core.at[i, slot] for i in range(cores - 1)]

    def hidden_of(block):
        return h_ref.at[pl.ds(pl.multiple_of(block * rows, rows), rows), :]

    order = []
    for t in range(line + 2):
        if t < line:
            order += [(0, t), (1, t)]
        if 0 <= t - 1 < line:
            order.append((2, t - 1))
        if 0 <= t - 2 < line:
            order.append((3, t - 2))
    order = [k * line + j for k, j in order]
    ahead = iter(range(4 * line))

    def give_next(count):
        for n in ahead:
            give(order[n], n)
            count -= 1
            if count == 0:
                break

    def take(ref, send_sem, recv_sem, peer):
        remote(sums.at[0], ref, send_sem, recv_sem, peer).wait_recv()
        return ref

    def take_a(n):
        return take(from_a.at[n], a_send.at[n], a_recv.at[n], to_a)

    give_next(2)
    for at, slot in enumerate(order):
        give_next(2)
        k, j = slot // line, slot % line
        refs = given(slot)
        if k < 2:
            add(own(slot), core, refs, sums.at[slot])
            send(sums.at[slot], from_a.at[slot], a_send.at[slot], a_recv.at[slot], to_a)
        elif k == 2:
            refs.append(take_a(j))
            add(own(slot), core, refs, sums.at[slot])
            send(sums.at[slot], from_b.at[j], b_send.at[j], b_recv.at[j], to_b)
        else:
            refs.append(take_a(line + j))
            refs.append(take(from_b.at[j], b_send.at[j], b_recv.at[j], to_b))
            if j < line - 1:
                add(own(slot), core, refs, sums.at[slot])
                send(sums.at[slot], from_z.at[j], z_send.at[j], z_recv.at[j], to_z[j])
            else:
                for i in range(line - 1):
                    refs.append(take(from_z.at[i], z_send.at[i], z_recv.at[i], to_z[i]))
                add(own(slot), core, refs, out_ref)
        if at == 2 * line - 1:
            for i in range(1, groups):
                peer = lax.rem(me + i, groups)
                send(hidden_of(peer), hid_ref.at[me], h_send.at[i - 1], h_recv.at[i - 1],
                     to_all[i - 1])
            kept = pltpu.make_async_copy(hidden_of(me), hid_ref.at[me], h_own)
            kept.start()
    for i in range(1, groups):
        peer = lax.rem(me - i + groups, groups)
        remote(hidden_of(me), hid_ref.at[peer], h_send.at[i - 1], h_recv.at[i - 1],
               to_all[i - 1]).wait_recv()
    kept.wait()
    for copy in started + list(pending.values()):
        copy.wait_send()


def scatter_sum(d_both, w_both, hidden, groups, cores):
    tokens, width = d_both.shape[0], w_both.shape[1]
    rows, wide, line = tokens // groups, width // cores, groups // 4
    dma = pltpu.SemaphoreType.DMA

    def slots(*count):
        return pltpu.VMEM((*count, rows, wide), jnp.bfloat16)

    return pl.pallas_call(
        functools.partial(scatter_kernel, groups, cores),
        out_shape=(
            jax.ShapeDtypeStruct((rows, wide), jnp.bfloat16),
            jax.ShapeDtypeStruct((groups, rows, hidden.shape[1]), hidden.dtype),
        ),
        in_specs=[
            pl.BlockSpec(memory_space=pltpu.VMEM), pl.BlockSpec(memory_space=pltpu.VMEM),
            pl.BlockSpec(memory_space=pl.ANY),
        ],
        out_specs=(
            pl.BlockSpec(memory_space=pltpu.VMEM), pl.BlockSpec(memory_space=pl.ANY),
        ),
        scratch_shapes=[
            slots(4 * line), slots(4, cores - 1), slots(cores - 1, 4 * line), slots(2 * line),
            slots(line), slots(line - 1),
            dma((cores - 1, 4 * line)), dma((cores - 1, 4 * line)),
            dma((2 * line,)), dma((2 * line,)),
            dma((line,)), dma((line,)),
            dma((line - 1,)), dma((line - 1,)),
            dma((groups - 1,)), dma((groups - 1,)), dma,
        ],
        compiler_params=pltpu.CompilerParams(collective_id=1, has_side_effects=True),
        name="scatter_sum",
    )(d_both, w_both, hidden)


def per_device(tokens, gate_codes, gate_scales, up_codes, up_scales, cotangent):
    groups = lax.axis_size("inter")
    whole, w_both = gather_tokens(
        tokens, gate_codes, gate_scales, up_codes, up_scales, groups, lax.axis_size("intra")
    )
    slabs, count, wide = whole.shape
    back = lax.all_to_all(cotangent, "inter", split_axis=1, concat_axis=0, tiled=True)
    owned = gate_codes.shape[0]

    def forward(weights):
        total = None
        for s in range(slabs):
            term = lax.dot_general(
                whole[s],
                weights[:, s * wide:(s + 1) * wide],
                (((1,), (1,)), ((), ())),
                preferred_element_type=jnp.float32,
            )
            total = term if total is None else total + term
        return total

    gate = forward(w_both[:owned])
    up = forward(w_both[owned:])
    sig = jax.nn.sigmoid(gate)
    act = gate * sig
    hidden = (act * up).astype(jnp.bfloat16)
    back = back.astype(jnp.float32)
    d_up = (back * act).astype(jnp.bfloat16)
    d_gate = (back * up * sig * (1.0 + gate * (1.0 - sig))).astype(jnp.bfloat16)
    token_grad, parts = scatter_sum(
        jnp.concatenate([d_gate, d_up], axis=1), w_both, hidden, groups, lax.axis_size("intra")
    )
    hidden = parts.transpose(1, 0, 2).reshape(parts.shape[1], groups * owned)

    def rows_grad(d_rows):
        terms = [
            lax.dot_general(
                d_rows, whole[s], (((0,), (0,)), ((), ())), preferred_element_type=jnp.float32
            )
            for s in range(slabs)
        ]
        return jnp.concatenate(terms, axis=1) / groups

    return (hidden, token_grad, rows_grad(d_gate), rows_grad(d_up))


def solution(mesh):
    return jax.shard_map(
        per_device,
        mesh=mesh,
        in_specs=(
            P("inter", "intra"),
            P(("intra", "inter"), None),
            P(("intra", "inter"), None),
            P(("intra", "inter"), None),
            P(("intra", "inter"), None),
            P("inter", "intra"),
        ),
        out_specs=(
            P("inter", "intra"),
            P("inter", "intra"),
            P(("intra", "inter"), None),
            P(("intra", "inter"), None),
        ),
        check_vma=False,
    )
```

```python
import functools

import jax
import jax.numpy as jnp
from jax import lax
from jax.experimental import pallas as pl
from jax.experimental.pallas import tpu as pltpu
from jax.sharding import PartitionSpec as P

MESH = pl.DeviceIdType.MESH


def place(groups):
    me = lax.axis_index("inter")
    core = lax.axis_index("intra")
    line = groups // 4
    return me, core, me // 4, line


def bits(me, parity):
    low, high = me % 2, (me // 2) % 2
    a = low * (1 - parity) + high * parity
    b = high * (1 - parity) + low * parity
    return a, b, 1 + parity, 2 - parity


def block_of(z, a, b, stride_a, stride_b):
    return z * 4 + a * stride_a + b * stride_b


def greet(peers):
    barrier = pltpu.get_barrier_semaphore()
    for peer in peers:
        pl.semaphore_signal(barrier, inc=1, device_id=peer, device_id_type=MESH)
    pl.semaphore_wait(barrier, len(peers))


def peers_of(me, core, z, line, cores, a, b, sa, sb):
    to_a = {"inter": block_of(z, 1 - a, b, sa, sb)}
    to_b = {"inter": block_of(z, a, 1 - b, sa, sb)}
    to_z = [{"inter": block_of(lax.rem(z + j, line), a, b, sa, sb)} for j in range(1, line)]
    to_core = [{"intra": lax.rem(core + i, cores)} for i in range(1, cores)]
    return to_a, to_b, to_z, to_core


def gather_kernel(groups, cores, x_ref, gc_ref, gs_ref, uc_ref, us_ref, out_ref, w_ref, own_sem, *sems):
    me, core, z, line = place(groups)
    a, b, sa, sb = bits(me, core % 2)
    rows, wide = x_ref.shape
    to_a, to_b, to_z, to_core = peers_of(me, core, z, line, cores, a, b, sa, sb)
    greet([to_a, to_b] + to_z + to_core)
    up_send, down_send, z_recv, b_send, b_recv, a_send, a_recv, c_send, c_recv = sems

    def at(slab, block):
        return out_ref.at[
            pl.ds(pl.multiple_of(block * rows, rows), rows),
            pl.ds(pl.multiple_of(slab * wide, wide), wide),
        ]

    def copy_of(src, slab, block, send_sem, recv_sem, peer):
        return pltpu.make_async_remote_copy(
            src_ref=src, dst_ref=at(slab, block), send_sem=send_sem, recv_sem=recv_sem,
            device_id=peer, device_id_type=MESH,
        )

    def block(k, zz, parity=None):
        pa, pb, psa, psb = bits(me, core % 2 if parity is None else parity)
        return block_of(zz, 1 - pa if k >= 2 else pa, 1 - pb if k % 2 else pb, psa, psb)

    up = {"inter": block_of(lax.rem(z + 1, line), a, b, sa, sb)}
    down = {"inter": block_of(lax.rem(z - 1 + line, line), a, b, sa, sb)}

    def to_a_copy(src, k, zz):
        return copy_of(src, core, block(k, zz), a_send.at[k, zz], a_recv.at[k, zz], to_a)

    def to_b_copy(src, zz):
        return copy_of(src, core, block(0, zz), b_send.at[zz], b_recv.at[zz], to_b)

    def core_copies(src, k, zz):
        return [
            copy_of(src, core, block(k, zz), c_send.at[i, k, zz], c_recv.at[i, k, zz], peer)
            for i, peer in enumerate(to_core)
        ]

    def line_copy(src, zz, upward):
        sems_of, peer = (up_send, up) if upward else (down_send, down)
        return copy_of(src, core, block(0, zz), sems_of.at[zz], z_recv.at[zz], peer)

    def begin(copies):
        for copy in copies:
            copy.start()

    own = pltpu.make_async_copy(x_ref, at(core, me), own_sem)

    @pl.when(z < line - 1)
    def _():
        line_copy(x_ref, z, True).start()

    @pl.when(z > 0)
    def _():
        line_copy(x_ref, z, False).start()

    begin([to_b_copy(x_ref, z), to_a_copy(x_ref, 0, z)] + core_copies(x_ref, 0, z))
    own.start()

    owned, blocks = gs_ref.shape
    step = gc_ref.shape[1] // blocks
    for first, codes, scales in ((0, gc_ref, gs_ref), (owned, uc_ref, us_ref)):
        for blk in range(blocks):
            values = codes[:, blk * step:(blk + 1) * step].astype(jnp.float32)
            values = values * scales[:, blk:blk + 1]
            w_ref[first:first + owned, blk * step:(blk + 1) * step] = values.astype(w_ref.dtype)

    def take_b(zz):
        src = at(core, block(1, zz))
        copy_of(x_ref, core, block(1, zz), b_send.at[zz], b_recv.at[zz], to_b).wait_recv()
        begin([to_a_copy(src, 1, zz)] + core_copies(src, 1, zz))

    def take_a(zz):
        for k in (2, 3):
            src = at(core, block(k, zz))
            copy_of(x_ref, core, block(k, zz), a_send.at[k - 2, zz], a_recv.at[k - 2, zz],
                    to_a).wait_recv()
            begin(core_copies(src, k, zz))

    def take_line(zz, upward):
        src = at(core, block(0, zz))
        line_copy(x_ref, zz, upward).wait_recv()

        @pl.when(z < line - 1 if upward else z > 0)
        def _():
            line_copy(src, zz, upward).start()

        begin([to_b_copy(src, zz), to_a_copy(src, 0, zz)] + core_copies(src, 0, zz))

    def nearby(shift, act):
        @pl.when(z >= shift)
        def _():
            act(z - shift, True)

        @pl.when(z + shift < line)
        def _():
            act(z + shift, False)

    take_b(z)
    for shift in range(1, line):
        nearby(shift, take_line)
        if shift == 1:
            take_a(z)
        else:
            nearby(shift - 1, lambda zz, _: take_a(zz))
        nearby(shift, lambda zz, _: take_b(zz))
    if line == 1:
        take_a(z)
    else:
        nearby(line - 1, lambda zz, _: take_a(zz))
    for i in range(1, cores):
        other = lax.rem(core - i + cores, cores)
        for k in range(4):
            for zz in range(line):
                copy_of(x_ref, other, block(k, zz, other % 2), c_send.at[i - 1, k, zz],
                        c_recv.at[i - 1, k, zz], to_core[i - 1]).wait_recv()
    own.wait()
    for zz in range(line):
        to_b_copy(x_ref, zz).wait_send()
        for k in range(2):
            to_a_copy(x_ref, k, zz).wait_send()
        for k in range(4):
            for copy in core_copies(x_ref, k, zz):
                copy.wait_send()

        @pl.when((zz <= z) & (z < line - 1))
        def _():
            line_copy(x_ref, zz, True).wait_send()

        @pl.when((zz >= z) & (z > 0))
        def _():
            line_copy(x_ref, zz, False).wait_send()


def gather_tokens(tokens, gate_codes, gate_scales, up_codes, up_scales, groups, cores):
    rows, wide = tokens.shape
    line = groups // 4
    dma = pltpu.SemaphoreType.DMA
    return pl.pallas_call(
        functools.partial(gather_kernel, groups, cores),
        out_shape=(
            jax.ShapeDtypeStruct((groups * rows, cores * wide), tokens.dtype),
            jax.ShapeDtypeStruct((2 * gate_codes.shape[0], gate_codes.shape[1]), jnp.bfloat16),
        ),
        in_specs=[pl.BlockSpec(memory_space=pl.ANY)] + [pl.BlockSpec(memory_space=pltpu.VMEM)] * 4,
        out_specs=(
            pl.BlockSpec(memory_space=pl.ANY), pl.BlockSpec(memory_space=pltpu.VMEM),
        ),
        scratch_shapes=[
            dma,
            dma((line,)), dma((line,)), dma((line,)),
            dma((line,)), dma((line,)),
            dma((2, line)), dma((2, line)),
            dma((cores - 1, 4, line)), dma((cores - 1, 4, line)),
        ],
        compiler_params=pltpu.CompilerParams(collective_id=0, has_side_effects=True),
        name="gather_tokens",
    )(tokens, gate_codes, gate_scales, up_codes, up_scales)


def scatter_kernel(groups, cores, d_ref, w_ref, h_ref, out_ref, hid_ref, sums, outbox,
                   from_core, from_a, from_b, from_z, *sems):
    me, core, z, line = place(groups)
    a, b, sa, sb = bits(me, core % 2)
    rows, wide = out_ref.shape
    to_a, to_b, to_z, to_core = peers_of(me, core, z, line, cores, a, b, sa, sb)
    to_all = [{"inter": lax.rem(me + i, groups)} for i in range(1, groups)]
    greet(to_all + to_core)
    (c_send, c_recv, a_send, a_recv, b_send, b_recv, z_send, z_recv, h_send, h_recv,
     h_own) = sems
    ring = outbox.shape[0]
    tile = min(512, wide)

    def block_at(parity, k, j):
        pa, pb, psa, psb = bits(me, parity)
        aa = 1 - pa if k < 2 else pa
        bb = 1 - pb if k % 2 == 0 else pb
        return block_of(lax.rem(z + 1 + j, line), aa, bb, psa, psb)

    started = []

    def remote(src, dst, send_sem, recv_sem, peer):
        return pltpu.make_async_remote_copy(
            src_ref=src, dst_ref=dst, send_sem=send_sem, recv_sem=recv_sem,
            device_id=peer, device_id_type=MESH,
        )

    def send(*args):
        copy = remote(*args)
        copy.start()
        started.append(copy)

    def add(block, slab, refs, dst):
        here = pl.ds(pl.multiple_of(block * rows, rows), rows)

        def body(t, _):
            cols = pl.ds(pl.multiple_of(t * tile, tile), tile)
            total = jnp.dot(
                d_ref[here, :],
                w_ref[:, pl.ds(pl.multiple_of(slab * wide + t * tile, tile), tile)],
                preferred_element_type=jnp.float32,
            )
            for ref in refs:
                total = total + ref[:, cols].astype(jnp.float32)
            dst[:, cols] = total.astype(dst.dtype)
            return 0

        lax.fori_loop(0, wide // tile, body, 0)

    pending = {}

    def give(slot, n):
        k, j = slot // line, slot % line
        for i in range(1, cores):
            other = lax.rem(core + i, cores)
            box = outbox.at[n % ring, i - 1]
            if (n % ring, i) in pending:
                pending[n % ring, i].wait_send()
            add(block_at(other % 2, k, j), other, [], box)
            copy = remote(box, from_core.at[i - 1, slot], c_send.at[i - 1, slot],
                          c_recv.at[i - 1, slot], to_core[i - 1])
            copy.start()
            pending[n % ring, i] = copy

    def own(slot):
        return block_at(core % 2, slot // line, slot % line)

    def given(slot):
        for i in range(cores - 1):
            remote(outbox.at[0, i], from_core.at[i, slot], c_send.at[i, slot], c_recv.at[i, slot],
                   to_core[i]).wait_recv()
        return [from_core.at[i, slot] for i in range(cores - 1)]

    def hidden_of(block):
        return h_ref.at[pl.ds(pl.multiple_of(block * rows, rows), rows), :]

    order = []
    for t in range(line + 2):
        if t < line:
            order += [(0, t), (1, t)]
        if 0 <= t - 1 < line:
            order.append((2, t - 1))
        if 0 <= t - 2 < line:
            order.append((3, t - 2))
    order = [k * line + j for k, j in order]
    ahead = iter(range(4 * line))

    def give_next(count):
        for n in ahead:
            give(order[n], n)
            count -= 1
            if count == 0:
                break

    def take(ref, send_sem, recv_sem, peer):
        remote(sums.at[0], ref, send_sem, recv_sem, peer).wait_recv()
        return ref

    def take_a(n):
        return take(from_a.at[n], a_send.at[n], a_recv.at[n], to_a)

    give_next(2)
    for at, slot in enumerate(order):
        give_next(2)
        k, j = slot // line, slot % line
        refs = given(slot)
        if k < 2:
            add(own(slot), core, refs, sums.at[slot])
            send(sums.at[slot], from_a.at[slot], a_send.at[slot], a_recv.at[slot], to_a)
        elif k == 2:
            refs.append(take_a(j))
            add(own(slot), core, refs, sums.at[slot])
            send(sums.at[slot], from_b.at[j], b_send.at[j], b_recv.at[j], to_b)
        else:
            refs.append(take_a(line + j))
            refs.append(take(from_b.at[j], b_send.at[j], b_recv.at[j], to_b))
            if j < line - 1:
                add(own(slot), core, refs, sums.at[slot])
                send(sums.at[slot], from_z.at[j], z_send.at[j], z_recv.at[j], to_z[j])
            else:
                for i in range(line - 1):
                    refs.append(take(from_z.at[i], z_send.at[i], z_recv.at[i], to_z[i]))
                add(own(slot), core, refs, out_ref)
        if at == 2 * line - 1:
            for i in range(1, groups):
                peer = lax.rem(me + i, groups)
                send(hidden_of(peer), hid_ref.at[me], h_send.at[i - 1], h_recv.at[i - 1],
                     to_all[i - 1])
            kept = pltpu.make_async_copy(hidden_of(me), hid_ref.at[me], h_own)
            kept.start()
    for i in range(1, groups):
        peer = lax.rem(me - i + groups, groups)
        remote(hidden_of(me), hid_ref.at[peer], h_send.at[i - 1], h_recv.at[i - 1],
               to_all[i - 1]).wait_recv()
    kept.wait()
    for copy in started + list(pending.values()):
        copy.wait_send()


def scatter_sum(d_both, w_both, hidden, groups, cores):
    tokens, width = d_both.shape[0], w_both.shape[1]
    rows, wide, line = tokens // groups, width // cores, groups // 4
    dma = pltpu.SemaphoreType.DMA

    def slots(*count):
        return pltpu.VMEM((*count, rows, wide), jnp.bfloat16)

    return pl.pallas_call(
        functools.partial(scatter_kernel, groups, cores),
        out_shape=(
            jax.ShapeDtypeStruct((rows, wide), jnp.bfloat16),
            jax.ShapeDtypeStruct((groups, rows, hidden.shape[1]), hidden.dtype),
        ),
        in_specs=[
            pl.BlockSpec(memory_space=pltpu.VMEM), pl.BlockSpec(memory_space=pltpu.VMEM),
            pl.BlockSpec(memory_space=pl.ANY),
        ],
        out_specs=(
            pl.BlockSpec(memory_space=pltpu.VMEM), pl.BlockSpec(memory_space=pl.ANY),
        ),
        scratch_shapes=[
            slots(4 * line), slots(4, cores - 1), slots(cores - 1, 4 * line), slots(2 * line),
            slots(line), slots(line - 1),
            dma((cores - 1, 4 * line)), dma((cores - 1, 4 * line)),
            dma((2 * line,)), dma((2 * line,)),
            dma((line,)), dma((line,)),
            dma((line - 1,)), dma((line - 1,)),
            dma((groups - 1,)), dma((groups - 1,)), dma,
        ],
        compiler_params=pltpu.CompilerParams(collective_id=1, has_side_effects=True),
        name="scatter_sum",
    )(d_both, w_both, hidden)


def per_device(tokens, gate_codes, gate_scales, up_codes, up_scales, cotangent):
    groups = lax.axis_size("inter")
    whole, w_both = gather_tokens(
        tokens, gate_codes, gate_scales, up_codes, up_scales, groups, lax.axis_size("intra")
    )
    back = lax.all_to_all(cotangent, "inter", split_axis=1, concat_axis=0, tiled=True)
    owned = gate_codes.shape[0]

    def forward(weights):
        return lax.dot_general(
            whole, weights, (((1,), (1,)), ((), ())), preferred_element_type=jnp.float32
        )

    gate = forward(w_both[:owned])
    up = forward(w_both[owned:])
    sig = jax.nn.sigmoid(gate)
    act = gate * sig
    hidden = (act * up).astype(jnp.bfloat16)
    back = back.astype(jnp.float32)
    d_up = (back * act).astype(jnp.bfloat16)
    d_gate = (back * up * sig * (1.0 + gate * (1.0 - sig))).astype(jnp.bfloat16)
    token_grad, parts = scatter_sum(
        jnp.concatenate([d_gate, d_up], axis=1), w_both, hidden, groups, lax.axis_size("intra")
    )
    hidden = parts.transpose(1, 0, 2).reshape(parts.shape[1], groups * owned)

    def rows_grad(d_rows):
        return lax.dot_general(
            d_rows, whole, (((0,), (0,)), ((), ())), preferred_element_type=jnp.float32
        ) / groups

    return (hidden, token_grad, rows_grad(d_gate), rows_grad(d_up))


def solution(mesh):
    return jax.shard_map(
        per_device,
        mesh=mesh,
        in_specs=(
            P("inter", "intra"),
            P(("intra", "inter"), None),
            P(("intra", "inter"), None),
            P(("intra", "inter"), None),
            P(("intra", "inter"), None),
            P("inter", "intra"),
        ),
        out_specs=(
            P("inter", "intra"),
            P("inter", "intra"),
            P(("intra", "inter"), None),
            P(("intra", "inter"), None),
        ),
        check_vma=False,
    )
```
